768 devices in a mesh: ctx: 48 (over y, z_lo, core), dp: 16 (over x, z_hi).
Axes of the slice: x: 4, y: 8, z: 12 (z_hi: 4, z_lo: 3; z = z_hi * 3 + z_lo), core: 2. Of those that a mesh axis runs over, the one named last changes fastest.
Arguments:
- q_proj: bfloat16 [16, 6144, 2048], P('dp', 'ctx'), may hold values from -6 to 6
- k_proj: bfloat16 [16, 6144, 2048], P('dp', 'ctx'), may hold values from -6 to 6
- v_proj: bfloat16 [16, 6144, 2048], P('dp', 'ctx'), may hold values from -6 to 6
- out_grad: bfloat16 [16, 6144, 2048], P('dp', 'ctx'), may hold values from -6 to 6
- contig_starts: int32 [16, 6144], P('dp', 'ctx'), may hold values 0 or 1
- filters: bfloat16 [128, 128], replicated, may hold values from -0.5 to 0.5
Outputs:
- mixed_out: bfloat16 [16, 6144, 2048], P('dp', 'ctx')
- grad_q: bfloat16 [16, 6144, 2048], P('dp', 'ctx')
- grad_k: bfloat16 [16, 6144, 2048], P('dp', 'ctx')
- grad_v: bfloat16 [16, 6144, 2048], P('dp', 'ctx')
- filter_grad: float32 [128, 128], replicated
The draws below stay inside these ranges and needn't reach their ends.
Inputs may be any that keep to these rules, and one draw needn't show every extreme that they name: `contig_starts`: a contig runs from a 1 to the token before the next 1 or to the end of its pack.
All inputs are finite; a program needn't handle non-finite values. No bound on the sum of `contig_starts` on one device may be relied on, other than what follows from the above.
Results may differ from the reference program's by a relative error of at most 0.0053.
Values may be sent and summed in bfloat16 or wider, within the bound.
A program may use at most 32 MiB of HBM per device.

```python
import math
import jax
import jax.numpy as jnp
from jax import lax

D = 2048
FILT = 128
GSIZE = 16
GROUPS = 128
R_DEV = 128
TOKENS = 6144
BATCH = 16


def touch_ends(result, stream_key, least, largest):
    dims = result.shape
    place = [jax.random.randint(jax.random.fold_in(stream_key, axis), (), 0, dims[axis]) for axis in range(len(dims))]
    result = result.at[tuple(place)].set(least)
    longest = dims.index(max(dims))
    place[longest] = (place[longest] + 1) % dims[longest]
    return result.at[tuple(place)].set(largest)


def block_scale(rng, extent, shards, low, high):
    loudness = 1.0
    for position, blocks in shards:
        heights = jax.random.uniform(jax.random.fold_in(jax.random.fold_in(rng, 6), position), (blocks,), jnp.float32, low / len(shards), high / len(shards))
        loudness = loudness * jnp.repeat(jnp.exp(heights), extent[position] // blocks).reshape((-1,) + (1,) * (len(extent) - 1 - position))
    return loudness


def gaussian(stream_key, extent, deviation, bound, split=(), held_as=jnp.bfloat16):
    level = block_scale(stream_key, extent, split, -0.22, 0.18) if split else 1.0
    values = jax.random.normal(stream_key, extent, jnp.float32) * deviation * level
    return jnp.minimum(jnp.maximum(values, -bound), bound).astype(held_as)


def setup_inputs(seed: int = 0) -> dict:
    seeds = jax.random.split(jax.random.key(seed), 7)
    q_proj = gaussian(seeds[0], (BATCH, TOKENS, D), 1.0, 6.0, ((0, 16), (1, 48)))
    k_proj = gaussian(seeds[1], (BATCH, TOKENS, D), 1.0, 6.0, ((0, 16), (1, 48)))
    v_proj = gaussian(seeds[2], (BATCH, TOKENS, D), 1.0, 6.0, ((0, 16), (1, 48)))
    out_grad = gaussian(seeds[3], (BATCH, TOKENS, D), 1.0, 6.0, ((0, 16), (1, 48)))
    contig_starts = touch_ends((jax.random.randint(seeds[4], (BATCH, TOKENS), 0, R_DEV) < 1).astype(jnp.int32), jax.random.fold_in(seeds[4], 1), 0, 1)
    filters = gaussian(seeds[5], (GROUPS, FILT), FILT ** -0.5, 0.5)
    return dict(q_proj=q_proj, k_proj=k_proj, v_proj=v_proj, out_grad=out_grad, contig_starts=contig_starts, filters=filters)


HIGH = lax.Precision.HIGHEST

def skew_rows(row_table):
    count = row_table.shape[0]
    tiled = jnp.tile(row_table, (1, FILT))[:, :FILT * (2 * FILT - 1)]
    return tiled.reshape(count, FILT, 2 * FILT - 1)

def diagonal_sums(products):
    lead = products.shape[:-2]
    flat = products.reshape(lead + (FILT * (2 * FILT - 1),))
    flat = jnp.concatenate([flat, jnp.zeros(lead + (FILT,), flat.dtype)], axis=-1)
    return lax.optimization_barrier(jnp.sum(flat.reshape(lead + (FILT, 2 * FILT))[..., :FILT], axis=-2))

def windows(extended):
    nblocks = extended.shape[0] // FILT - 1
    blocks = extended.reshape((nblocks + 1, FILT) + extended.shape[1:])
    return jnp.concatenate([blocks[:-1], blocks[1:, :FILT - 1]], axis=1)

def intersection_add(pieces):
    nblocks = pieces.shape[0]
    first = pieces[:, :FILT]
    second = jnp.concatenate([pieces[:, FILT:], jnp.zeros_like(pieces[:, :1])], axis=1)
    zero_block = jnp.zeros_like(first[:1])
    total = jnp.concatenate([first, zero_block], 0) + jnp.concatenate([zero_block, second], 0)
    return total.reshape(((nblocks + 1) * FILT,) + pieces.shape[2:])

def one_pack(items, base_table):
    q_row, k_row, v_row, dy_row, starts_row = items
    prod_kv = (k_row.astype(jnp.float32) * v_row.astype(jnp.float32)).astype(jnp.bfloat16)
    cotangent = (dy_row.astype(jnp.float32) * q_row.astype(jnp.float32)).astype(jnp.bfloat16)
    segment_ids = jnp.cumsum(starts_row).astype(jnp.int32)
    kv_ext = jnp.concatenate([jnp.zeros((FILT - 1, D), jnp.bfloat16), prod_kv, jnp.zeros((1, D), jnp.bfloat16)], 0)
    seg_ext = jnp.concatenate([jnp.full((FILT - 1,), -1, jnp.int32), segment_ids, jnp.full((1,), -1, jnp.int32)], 0)
    kv_win = windows(kv_ext)
    seg_win = windows(seg_ext)
    seg_own = segment_ids.reshape(-1, FILT)
    cot_blocks = cotangent.reshape(-1, FILT, D)
    span = 2 * FILT - 1

    def per_block(block_items):
        kv_w, seg_w, seg_o, cot_b = block_items
        linked = (seg_w[None, :] == seg_o[:, None]).astype(jnp.float32)
        table = base_table * linked[None]
        kv_wide = kv_w.astype(jnp.float32).reshape(span, GROUPS, GSIZE)
        conv = jnp.einsum('gts,sgc->tgc', table, kv_wide, precision=HIGH).reshape(FILT, D)
        cot_wide = cot_b.astype(jnp.float32).reshape(FILT, GROUPS, GSIZE)
        back = jnp.einsum('gts,tgc->sgc', table, cot_wide, precision=HIGH).reshape(span, D)
        products = jnp.einsum('tgc,sgc->gts', cot_wide, kv_wide, precision=HIGH) * linked[None]
        return (conv, back, diagonal_sums(products))
    conv, back, diag = lax.map(per_block, (kv_win, seg_win, seg_own, cot_blocks))
    conv = conv.reshape(TOKENS, D)
    grad_kv = intersection_add(back)[FILT - 1:FILT - 1 + TOKENS]
    mixed = (q_row.astype(jnp.float32) * conv).astype(jnp.bfloat16)
    grad_q = (dy_row.astype(jnp.float32) * conv).astype(jnp.bfloat16)
    grad_k = (grad_kv * v_row.astype(jnp.float32)).astype(jnp.bfloat16)
    grad_v = (grad_kv * k_row.astype(jnp.float32)).astype(jnp.bfloat16)
    return (mixed, grad_q, grad_k, grad_v, lax.optimization_barrier(jnp.sum(diag, axis=0)))

def reference(q_proj, k_proj, v_proj, out_grad, contig_starts, filters):
    taps = filters.astype(jnp.float32)
    base_table = skew_rows(jnp.concatenate([taps[:, ::-1], jnp.zeros_like(taps)], axis=1))
    mixed, grad_q, grad_k, grad_v, diag = lax.map(lambda items: one_pack(items, base_table), (q_proj, k_proj, v_proj, out_grad, contig_starts))
    scale = 1.0 / math.sqrt(BATCH * TOKENS * GSIZE)
    filter_grad = lax.optimization_barrier(jnp.sum(diag, axis=0))[:, ::-1] * scale
    return (mixed, grad_q, grad_k, grad_v, filter_grad)
```

```python
import functools
import math

import jax
import jax.numpy as jnp
from jax import lax
from jax.experimental import pallas as pl
from jax.experimental.pallas import tpu as pltpu
from jax.sharding import PartitionSpec as P

FILT = 128
GSIZE = 16
LANES = 128
PER_TILE = LANES // GSIZE
SUB = 8
CORES = 2
Z_LO = 3
Z_HI = 4
CHUNK = 4
MESH = pl.DeviceIdType.MESH
F32 = jnp.float32
BF16 = jnp.bfloat16


def ring_kernel(
    n_ctx,
    n_dp,
    scale,
    q_hbm,
    k_hbm,
    v_hbm,
    dy_hbm,
    starts_ref,
    filt_ref,
    mixed_hbm,
    gq_hbm,
    gk_hbm,
    gv_hbm,
    fg_ref,
    q,
    k,
    v,
    dy,
    kvx,
    cotx,
    kvs,
    cots,
    lhs,
    lane_mask,
    masks,
    pair_mask,
    fil,
    rfil,
    fold,
    filt_rev,
    filt_local,
    slots1,
    slots2,
    slots3,
    acc1,
    acc2,
    acc3,
    gathered,
    mixed,
    gq,
    gk,
    gv,
    in_sem,
    out_sem,
    kv_send,
    kv_recv,
    cot_send,
    cot_recv,
    s1_send,
    s1_recv,
    s2_send,
    s2_recv,
    s3_send,
    s3_recv,
    s4_send,
    s4_recv,
):
    ctx = lax.axis_index("ctx")
    dp = lax.axis_index("dp")
    core = lax.rem(ctx, CORES)
    z_lo = lax.rem(ctx // CORES, Z_LO)
    y = ctx // (CORES * Z_LO)
    z_hi = lax.rem(dp, Z_HI)
    x = dp // Z_HI
    n_y = n_ctx // (CORES * Z_LO)
    n_x = n_dp // Z_HI
    n_plane = n_x * CORES
    n_z = Z_LO * Z_HI
    me1 = x * CORES + core
    me3 = z_hi * Z_LO + z_lo
    tiles = kvx.shape[0]
    n_chunks = tiles // CHUNK
    share = filt_local.shape[0] // n_plane

    def plane_peer(p):
        return {"ctx": ctx - core + lax.rem(p, CORES), "dp": (p // CORES) * Z_HI + z_hi}

    def y_peer(p):
        return {"ctx": p * (CORES * Z_LO) + z_lo * CORES + core, "dp": dp}

    def z_peer(p):
        return {
            "ctx": y * (CORES * Z_LO) + lax.rem(p, Z_LO) * CORES + core,
            "dp": x * Z_HI + p // Z_LO,
        }

    nxt = {"ctx": lax.rem(ctx + 1, n_ctx), "dp": dp}
    prv = {"ctx": lax.rem(ctx + n_ctx - 1, n_ctx), "dp": dp}

    loads = [
        pltpu.make_async_copy(src, dst, in_sem.at[i])
        for i, (src, dst) in enumerate(((k_hbm, k), (v_hbm, v), (q_hbm, q), (dy_hbm, dy)))
    ]
    for copy in loads:
        copy.start()

    barrier = pltpu.get_barrier_semaphore()

    def greet(device):
        pl.semaphore_signal(barrier, inc=1, device_id=device, device_id_type=MESH)

    def greet_all(n, me, peer):
        def one(d, carry):
            greet(peer(lax.rem(me + d, n)))
            return carry

        lax.fori_loop(1, n, one, 0)

    greet(nxt)
    greet(prv)
    greet_all(n_z, me3, z_peer)
    greet_all(n_y, y, y_peer)
    greet_all(n_plane, me1, plane_peer)

    row = lax.broadcasted_iota(jnp.int32, (FILT, FILT), 0)
    col = lax.broadcasted_iota(jnp.int32, (FILT, FILT), 1)
    starts = starts_ref[...].astype(F32)
    seg_row = jnp.broadcast_to(
        jnp.sum(jnp.where(col <= row, starts, 0.0), axis=1, keepdims=True), (FILT, FILT)
    )
    seg_col = seg_row.T
    last = jnp.sum(starts)
    same = seg_row == seg_col
    fresh = seg_row == 0.0
    final = seg_row == last

    def held(cond):
        return jnp.where(cond, 1.0, 0.0)

    low = held(same & (col <= row))
    high = held(fresh & (col > row))
    pair_mask[...] = low + high
    masks[0] = high.astype(BF16)
    masks[1] = low.astype(BF16)
    masks[2] = held(same & (row <= col)).astype(BF16)
    masks[3] = held(final & (col < row)).astype(BF16)
    masks[4] = (held(final) * jnp.where(ctx == n_ctx - 1, 0.0, 1.0)).astype(BF16)
    masks[5] = (held(fresh) * jnp.where(ctx == 0, 0.0, 1.0)).astype(BF16)
    lane_group = col // GSIZE
    for g in range(PER_TILE):
        lane_mask[g] = held(lane_group == g).astype(BF16)
    mirror = held(row == lax.rem(FILT - col, FILT))
    taps = filt_ref[...]
    fil[...] = taps.astype(F32)
    rfil[...] = jnp.dot(taps, mirror.astype(BF16), preferred_element_type=F32)

    def lanes_of(j):
        return pl.ds(pl.multiple_of(j * LANES, LANES), LANES)

    loads[0].wait()
    loads[1].wait()

    def make_kv(j, carry):
        lanes = lanes_of(j)
        prod = (k[:, lanes].astype(F32) * v[:, lanes].astype(F32)).astype(BF16)
        kvx[j, FILT:, :] = prod
        kvs[j] = prod * masks[4]
        return carry

    lax.fori_loop(0, tiles, make_kv, 0)

    pl.semaphore_wait(barrier, 2 + (n_z - 1) + (n_y - 1) + (n_plane - 1))

    def kv_copy(i):
        part = pl.ds(i * CHUNK, CHUNK)
        return pltpu.make_async_remote_copy(
            src_ref=kvs.at[part],
            dst_ref=kvx.at[part, 0:FILT, :],
            send_sem=kv_send.at[i],
            recv_sem=kv_recv.at[i],
            device_id=nxt,
            device_id_type=MESH,
        )

    def cot_copy(i):
        part = pl.ds(i * CHUNK, CHUNK)
        return pltpu.make_async_remote_copy(
            src_ref=cots.at[part],
            dst_ref=cotx.at[part, FILT:, :],
            send_sem=cot_send.at[i],
            recv_sem=cot_recv.at[i],
            device_id=prv,
            device_id_type=MESH,
        )

    for i in range(n_chunks):
        kv_copy(i).start()

    loads[2].wait()
    loads[3].wait()

    def make_cot(j, carry):
        lanes = lanes_of(j)
        prod = (dy[:, lanes].astype(F32) * q[:, lanes].astype(F32)).astype(BF16)
        cotx[j, 0:FILT, :] = prod
        cots[j] = prod * masks[5]
        return carry

    lax.fori_loop(0, tiles, make_cot, 0)

    def products(j, carry):
        cot = cotx[j, 0:FILT, :]
        for g in range(PER_TILE):
            lhs[g * FILT : (g + 1) * FILT, 0:LANES] = cot * lane_mask[g]
        pairs = lax.dot_general(
            lhs[:, 0:LANES], kvx[j], (((1,), (1,)), ((), ())), preferred_element_type=F32
        )
        for g in range(PER_TILE):
            block = pairs[g * FILT : (g + 1) * FILT]
            square = jnp.where(col <= row, block[:, FILT:], block[:, :FILT]) * pair_mask[...]
            folded = square[0:SUB]
            for a in range(1, FILT // SUB):
                folded = folded + pltpu.roll(square[a * SUB : (a + 1) * SUB], FILT - a * SUB, 1)
            fold[g] = folded
        taps8 = fold[:, 0, :]
        for b in range(1, SUB):
            taps8 = taps8 + pltpu.roll(fold[:, b, :], FILT - b, 1)
        filt_rev[pl.ds(pl.multiple_of(j * PER_TILE, PER_TILE), PER_TILE), :] = taps8
        return carry

    for i in range(n_chunks):
        kv_copy(i).wait_recv()
        if i == n_chunks - 1:
            for c in range(n_chunks):
                cot_copy(c).start()
        lax.fori_loop(i * CHUNK, (i + 1) * CHUNK, products, 0)

    filt_local[...] = lax.dot_general(
        filt_rev[...],
        mirror,
        (((1,), (0,)), ((), ())),
        precision=lax.Precision.HIGHEST,
        preferred_element_type=F32,
    )

    def send_all(n, me, peer, src_of, dst, send, recv):
        def one(d, carry):
            p = lax.rem(me + d, n)
            pltpu.make_async_remote_copy(
                src_ref=src_of(p),
                dst_ref=dst(me),
                send_sem=send.at[p],
                recv_sem=recv.at[me],
                device_id=peer(p),
                device_id_type=MESH,
            ).start()
            return carry

        lax.fori_loop(1, n, one, 0)

    def await_all(n, me, peer, src_of, dst, send, recv, sent):
        def one(d, carry):
            p = lax.rem(me + d, n)
            copy = pltpu.make_async_remote_copy(
                src_ref=src_of(p),
                dst_ref=dst(p),
                send_sem=send.at[p],
                recv_sem=recv.at[p],
                device_id=peer(p),
                device_id_type=MESH,
            )
            if sent:
                copy.wait_send()
            else:
                copy.wait_recv()
            return carry

        lax.fori_loop(1, n, one, 0)

    def share_of(ref, p):
        return ref.at[pl.ds(pl.multiple_of(p * share, share), share)]

    stage1 = (n_plane, me1, plane_peer, lambda p: share_of(filt_local, p), lambda p: slots1.at[p], s1_send, s1_recv)
    stage2 = (n_y, y, y_peer, lambda p: acc1, lambda p: slots2.at[p], s2_send, s2_recv)
    stage3 = (n_z, me3, z_peer, lambda p: acc2, lambda p: slots3.at[p], s3_send, s3_recv)
    stage4 = (n_plane, me1, plane_peer, lambda p: acc3, lambda p: share_of(gathered, p), s4_send, s4_recv)

    def total(slots, n):
        result = slots[0]
        for i in range(1, n):
            result = result + slots[i]
        return result

    lane_of = lax.broadcasted_iota(jnp.int32, (FILT, LANES), 1) // GSIZE

    def table(rows8, first, second):
        for g in range(PER_TILE):
            base = jnp.broadcast_to(rows8[g : g + 1, :], (FILT, FILT))
            circ = pltpu.roll(base, 0, 1, stride=1, stride_axis=0).astype(BF16)
            lhs[g * FILT : (g + 1) * FILT, 0:FILT] = circ * masks[first]
            lhs[g * FILT : (g + 1) * FILT, FILT:] = circ * masks[second]

    def apply_table(operand):
        result = jnp.dot(lhs[...], operand, preferred_element_type=F32)
        out = result[0:FILT]
        for g in range(1, PER_TILE):
            out = jnp.where(lane_of == g, result[g * FILT : (g + 1) * FILT], out)
        return out

    def forward(j, carry):
        lanes = lanes_of(j)
        rows8 = rfil[pl.ds(pl.multiple_of(j * PER_TILE, PER_TILE), PER_TILE), :]
        table(rows8, 0, 1)
        conv = apply_table(kvx[j])
        mixed[:, lanes] = (q[:, lanes].astype(F32) * conv).astype(BF16)
        gq[:, lanes] = (dy[:, lanes].astype(F32) * conv).astype(BF16)
        return carry

    def backward(j, carry):
        lanes = lanes_of(j)
        rows8 = fil[pl.ds(pl.multiple_of(j * PER_TILE, PER_TILE), PER_TILE), :]
        table(rows8, 2, 3)
        grad = apply_table(cotx[j])
        gk[:, lanes] = (v[:, lanes].astype(F32) * grad).astype(BF16)
        gv[:, lanes] = (k[:, lanes].astype(F32) * grad).astype(BF16)
        return carry

    send_all(*stage1)
    slots1[me1] = filt_local[pl.ds(pl.multiple_of(me1 * share, share), share), :]
    lax.fori_loop(0, tiles // 2, forward, 0)
    await_all(*stage1, False)
    acc1[...] = total(slots1, n_plane)
    send_all(*stage2)
    slots2[y] = acc1[...]
    lax.fori_loop(tiles // 2, tiles, forward, 0)
    stores = [
        pltpu.make_async_copy(src, dst, out_sem.at[i])
        for i, (src, dst) in enumerate(((mixed, mixed_hbm), (gq, gq_hbm), (gk, gk_hbm), (gv, gv_hbm)))
    ]
    stores[0].start()
    stores[1].start()
    await_all(*stage2, False)
    acc2[...] = total(slots2, n_y)
    send_all(*stage3)
    slots3[me3] = acc2[...]
    for i in range(n_chunks):
        cot_copy(i).wait_recv()
        lax.fori_loop(i * CHUNK, (i + 1) * CHUNK, backward, 0)
    stores[2].start()
    stores[3].start()
    await_all(*stage3, False)
    acc3[...] = total(slots3, n_z)
    send_all(*stage4)
    gathered[pl.ds(pl.multiple_of(me1 * share, share), share), :] = acc3[...]
    for i in range(n_chunks):
        kv_copy(i).wait_send()
        cot_copy(i).wait_send()
    await_all(*stage1, True)
    await_all(*stage2, True)
    await_all(*stage3, True)
    for copy in stores:
        copy.wait()
    await_all(*stage4, False)
    fg_ref[...] = gathered[...] * scale
    await_all(*stage4, True)


def per_device(n_ctx, n_dp, q_proj, k_proj, v_proj, out_grad, contig_starts, filters):
    rows, width = q_proj.shape[1:]
    groups = filters.shape[0]
    tiles = width // LANES
    n_y = n_ctx // (CORES * Z_LO)
    n_plane = (n_dp // Z_HI) * CORES
    n_z = Z_LO * Z_HI
    share = groups // n_plane
    n_chunks = tiles // CHUNK
    scale = 1.0 / math.sqrt(rows * n_ctx * n_dp * GSIZE)
    any_spec = pl.BlockSpec(memory_space=pl.ANY)
    vmem_spec = pl.BlockSpec(memory_space=pltpu.VMEM)
    big = jax.ShapeDtypeStruct((rows, width), BF16)
    dma = pltpu.SemaphoreType.DMA
    wide = pltpu.VMEM((rows, width), BF16)
    mixed, grad_q, grad_k, grad_v, filter_grad = pl.pallas_call(
        functools.partial(ring_kernel, n_ctx, n_dp, scale),
        out_shape=(big, big, big, big, jax.ShapeDtypeStruct((groups, FILT), F32)),
        in_specs=[any_spec] * 4 + [vmem_spec] * 2,
        out_specs=(any_spec, any_spec, any_spec, any_spec, vmem_spec),
        scratch_shapes=[
            wide,
            wide,
            wide,
            wide,
            pltpu.VMEM((tiles, 2 * FILT, LANES), BF16),
            pltpu.VMEM((tiles, 2 * FILT, LANES), BF16),
            pltpu.VMEM((tiles, FILT, LANES), BF16),
            pltpu.VMEM((tiles, FILT, LANES), BF16),
            pltpu.VMEM((PER_TILE * FILT, 2 * FILT), BF16),
            pltpu.VMEM((PER_TILE, FILT, LANES), BF16),
            pltpu.VMEM((6, FILT, FILT), BF16),
            pltpu.VMEM((FILT, FILT), F32),
            pltpu.VMEM((groups, FILT), F32),
            pltpu.VMEM((groups, FILT), F32),
            pltpu.VMEM((PER_TILE, SUB, FILT), F32),
            pltpu.VMEM((groups, FILT), F32),
            pltpu.VMEM((groups, FILT), F32),
            pltpu.VMEM((n_plane, share, FILT), F32),
            pltpu.VMEM((n_y, share, FILT), F32),
            pltpu.VMEM((n_z, share, FILT), F32),
            pltpu.VMEM((share, FILT), F32),
            pltpu.VMEM((share, FILT), F32),
            pltpu.VMEM((share, FILT), F32),
            pltpu.VMEM((groups, FILT), F32),
            wide,
            wide,
            wide,
            wide,
            dma((4,)),
            dma((4,)),
            dma((n_chunks,)),
            dma((n_chunks,)),
            dma((n_chunks,)),
            dma((n_chunks,)),
            dma((n_plane,)),
            dma((n_plane,)),
            dma((n_y,)),
            dma((n_y,)),
            dma((n_z,)),
            dma((n_z,)),
            dma((n_plane,)),
            dma((n_plane,)),
        ],
        compiler_params=pltpu.CompilerParams(collective_id=0, has_side_effects=True),
    )(q_proj[0], k_proj[0], v_proj[0], out_grad[0], contig_starts, filters)
    return (mixed[None], grad_q[None], grad_k[None], grad_v[None], filter_grad)


def solution(mesh):
    split = P("dp", "ctx", None)
    return jax.shard_map(
        functools.partial(per_device, mesh.shape["ctx"], mesh.shape["dp"]),
        mesh=mesh,
        in_specs=(split, split, split, split, P("dp", "ctx"), P()),
        out_specs=(split, split, split, split, P()),
        check_vma=False,
    )
```

```python
import functools
import math

import jax
import jax.numpy as jnp
from jax import lax
from jax.experimental import pallas as pl
from jax.experimental.pallas import tpu as pltpu
from jax.sharding import PartitionSpec as P

FILT = 128
GSIZE = 16
LANES = 128
PER_TILE = LANES // GSIZE
SUB = 8
CORES = 2
Z_LO = 3
Z_HI = 4
CHUNK = 2
COT_CHUNK = 4
PARTS = 2
MESH = pl.DeviceIdType.MESH
F32 = jnp.float32
BF16 = jnp.bfloat16


def ring_kernel(
    n_ctx,
    n_dp,
    scale,
    q_hbm,
    k_hbm,
    v_hbm,
    dy_hbm,
    starts_ref,
    filt_ref,
    mixed,
    gq,
    gk,
    gv,
    fg_ref,
    q,
    k,
    v,
    dy,
    kvx,
    cotx,
    kvs,
    cots,
    lhs,
    lane_mask,
    masks,
    pair_mask,
    fil,
    rfil,
    fold,
    filt_rev,
    filt_local,
    slots1,
    slots2,
    slots3,
    acc1,
    acc2,
    acc3,
    gathered,
    in_sem,
    kv_send,
    kv_recv,
    cot_send,
    cot_recv,
    s1_send,
    s1_recv,
    s2_send,
    s2_recv,
    s3_send,
    s3_recv,
    s4_send,
    s4_recv,
    heard,
):
    ctx = lax.axis_index("ctx")
    dp = lax.axis_index("dp")
    core = lax.rem(ctx, CORES)
    z_lo = lax.rem(ctx // CORES, Z_LO)
    y = ctx // (CORES * Z_LO)
    z_hi = lax.rem(dp, Z_HI)
    x = dp // Z_HI
    n_y = n_ctx // (CORES * Z_LO)
    n_x = n_dp // Z_HI
    n_plane = n_x * CORES
    n_z = Z_LO * Z_HI
    me1 = x * CORES + core
    me3 = z_hi * Z_LO + z_lo
    tiles = kvx.shape[0]
    n_chunks = tiles // CHUNK
    n_cot = tiles // COT_CHUNK
    share = filt_local.shape[0] // (n_plane * PARTS)
    part_groups = filt_local.shape[0] // PARTS
    part_chunks = n_chunks // PARTS

    def plane_peer(p):
        return {"ctx": ctx - core + lax.rem(p, CORES), "dp": (p // CORES) * Z_HI + z_hi}

    def y_peer(p):
        return {"ctx": p * (CORES * Z_LO) + z_lo * CORES + core, "dp": dp}

    def z_peer(p):
        return {
            "ctx": y * (CORES * Z_LO) + lax.rem(p, Z_LO) * CORES + core,
            "dp": x * Z_HI + p // Z_LO,
        }

    nxt = {"ctx": lax.rem(ctx + 1, n_ctx), "dp": dp}
    prv = {"ctx": lax.rem(ctx + n_ctx - 1, n_ctx), "dp": dp}

    loads = [
        pltpu.make_async_copy(src, dst, in_sem.at[i])
        for i, (src, dst) in enumerate(((k_hbm, k), (v_hbm, v), (q_hbm, q), (dy_hbm, dy)))
    ]
    for copy in loads:
        copy.start()

    barrier = pltpu.get_barrier_semaphore()

    def greet(device):
        pl.semaphore_signal(barrier, inc=1, device_id=device, device_id_type=MESH)

    def greet_all(n, me, peer):
        def one(d, carry):
            greet(peer(lax.rem(me + d, n)))
            return carry

        lax.fori_loop(1, n, one, 0)

    def z_step(d):
        return z_peer(lax.rem(me3 + d + n_z, n_z))

    z_near = [d for d in (1, -1) if n_z > 1]
    z_far = [d for d in (2, -2) if n_z > 3]
    greet_all(n_y, y, y_peer)
    greet(nxt)
    greet(prv)
    for d in z_near:
        greet(z_step(d))
    greet_all(n_plane, me1, plane_peer)

    def tell(stage, steps):
        for d in steps:
            pl.semaphore_signal(
                heard.at[stage], inc=1, device_id=z_step(d), device_id_type=MESH
            )

    def hear(stage, steps):
        if steps:
            pl.semaphore_wait(heard.at[stage], len(steps))

    row = lax.broadcasted_iota(jnp.int32, (FILT, FILT), 0)
    col = lax.broadcasted_iota(jnp.int32, (FILT, FILT), 1)
    starts = starts_ref[...].astype(F32)
    seg_row = jnp.broadcast_to(
        jnp.sum(jnp.where(col <= row, starts, 0.0), axis=1, keepdims=True), (FILT, FILT)
    )
    seg_col = seg_row.T
    last = jnp.sum(starts)
    same = seg_row == seg_col
    fresh = seg_row == 0.0
    final = seg_row == last

    def held(cond):
        return jnp.where(cond, 1.0, 0.0)

    low = held(same & (col <= row))
    high = held(fresh & (col > row))
    pair_mask[...] = low + high
    masks[0] = high.astype(BF16)
    masks[1] = low.astype(BF16)
    masks[2] = held(same & (row <= col)).astype(BF16)
    masks[3] = held(final & (col < row)).astype(BF16)
    masks[4] = (held(final) * jnp.where(ctx == n_ctx - 1, 0.0, 1.0)).astype(BF16)
    masks[5] = (held(fresh) * jnp.where(ctx == 0, 0.0, 1.0)).astype(BF16)
    lane_group = col // GSIZE
    for g in range(PER_TILE):
        lane_mask[g] = held(lane_group == g).astype(BF16)
    mirror = held(row == lax.rem(FILT - col, FILT))
    taps = filt_ref[...]
    fil[...] = taps.astype(F32)
    rfil[...] = jnp.dot(taps, mirror.astype(BF16), preferred_element_type=F32)

    def lanes_of(j):
        return pl.ds(pl.multiple_of(j * LANES, LANES), LANES)

    loads[0].wait()
    loads[1].wait()

    def make_kv(j, carry):
        lanes = lanes_of(j)
        prod = (k[:, lanes].astype(F32) * v[:, lanes].astype(F32)).astype(BF16)
        kvx[j, FILT:, :] = prod
        kvs[j] = prod * masks[4]
        return carry

    lax.fori_loop(0, tiles, make_kv, 0)

    pl.semaphore_wait(barrier, 2 + len(z_near) + (n_y - 1) + (n_plane - 1))

    def kv_copy(i):
        part = pl.ds(i * CHUNK, CHUNK)
        return pltpu.make_async_remote_copy(
            src_ref=kvs.at[part],
            dst_ref=kvx.at[part, 0:FILT, :],
            send_sem=kv_send,
            recv_sem=kv_recv.at[i],
            device_id=nxt,
            device_id_type=MESH,
        )

    def cot_copy(i):
        part = pl.ds(i * COT_CHUNK, COT_CHUNK)
        return pltpu.make_async_remote_copy(
            src_ref=cots.at[part],
            dst_ref=cotx.at[part, FILT:, :],
            send_sem=cot_send,
            recv_sem=cot_recv.at[i],
            device_id=prv,
            device_id_type=MESH,
        )

    for i in range(n_chunks):
        kv_copy(i).start()
    tell(0, z_near)

    loads[2].wait()
    loads[3].wait()

    def make_cot(j, carry):
        lanes = lanes_of(j)
        prod = (dy[:, lanes].astype(F32) * q[:, lanes].astype(F32)).astype(BF16)
        cotx[j, 0:FILT, :] = prod
        cots[j] = prod * masks[5]
        return carry

    lax.fori_loop(0, tiles, make_cot, 0)

    def products(j, carry):
        cot = cotx[j, 0:FILT, :]
        for g in range(PER_TILE):
            lhs[g * FILT : (g + 1) * FILT, 0:LANES] = cot * lane_mask[g]
        pairs = lax.dot_general(
            lhs[:, 0:LANES], kvx[j], (((1,), (1,)), ((), ())), preferred_element_type=F32
        )
        for g in range(PER_TILE):
            block = pairs[g * FILT : (g + 1) * FILT]
            square = jnp.where(col <= row, block[:, FILT:], block[:, :FILT]) * pair_mask[...]
            folded = square[0:SUB]
            for a in range(1, FILT // SUB):
                folded = folded + pltpu.roll(square[a * SUB : (a + 1) * SUB], FILT - a * SUB, 1)
            fold[g] = folded
        taps8 = fold[:, 0, :]
        for b in range(1, SUB):
            taps8 = taps8 + pltpu.roll(fold[:, b, :], FILT - b, 1)
        filt_rev[pl.ds(pl.multiple_of(j * PER_TILE, PER_TILE), PER_TILE), :] = taps8
        return carry

    def send_all(h, n, me, peer, src_of, dst, landed, send, recv):
        def one(d, carry):
            p = lax.rem(me + d, n)
            pltpu.make_async_remote_copy(
                src_ref=src_of(h, p),
                dst_ref=dst(h, me),
                send_sem=send,
                recv_sem=recv.at[h],
                device_id=peer(p),
                device_id_type=MESH,
            ).start()
            return carry

        lax.fori_loop(1, n, one, 0)

    def everything(part, send, recv):
        return pltpu.make_async_remote_copy(
            src_ref=part,
            dst_ref=part,
            send_sem=send,
            recv_sem=recv,
            device_id=nxt,
            device_id_type=MESH,
        )

    def await_part(h, n, me, peer, src_of, dst, landed, send, recv):
        everything(landed.at[h, pl.ds(0, n - 1)], send, recv.at[h]).wait_recv()

    def await_sent(n, me, peer, src_of, dst, landed, send, recv):
        everything(landed.at[:, pl.ds(0, n - 1)], send, recv.at[0]).wait_send()

    def rows_of(h, p):
        return pl.ds(pl.multiple_of(h * part_groups + p * share, share), share)

    def share_of(ref):
        return lambda h, p: ref.at[rows_of(h, p)]

    def slot_of(ref):
        return lambda h, p: ref.at[h, p]

    def whole(ref):
        return lambda h, p: ref.at[h]

    stage1 = (n_plane, me1, plane_peer, share_of(filt_local), slot_of(slots1), slots1, s1_send, s1_recv)
    stage2 = (n_y, y, y_peer, whole(acc1), slot_of(slots2), slots2, s2_send, s2_recv)
    stage3 = (n_z, me3, z_peer, whole(acc2), slot_of(slots3), slots3, s3_send, s3_recv)
    stage4 = (n_plane, me1, plane_peer, whole(acc3), slot_of(gathered), gathered, s4_send, s4_recv)

    def total(slots, h, n):
        result = slots[h, 0]
        for i in range(1, n):
            result = result + slots[h, i]
        return result

    def begin(h):
        span = slice(h * part_groups, (h + 1) * part_groups)
        filt_local[span, :] = lax.dot_general(
            filt_rev[span, :],
            mirror,
            (((1,), (0,)), ((), ())),
            precision=lax.Precision.HIGHEST,
            preferred_element_type=F32,
        )
        send_all(h, *stage1)
        slots1[h, me1] = filt_local[rows_of(h, me1), :]

    def after1(h):
        await_part(h, *stage1)
        acc1[h] = total(slots1, h, n_plane)
        send_all(h, *stage2)
        slots2[h, y] = acc1[h]

    def after2(h):
        await_part(h, *stage2)
        acc2[h] = total(slots2, h, n_y)
        send_all(h, *stage3)
        slots3[h, me3] = acc2[h]

    def after3(h):
        await_part(h, *stage3)
        acc3[h] = total(slots3, h, n_z)
        send_all(h, *stage4)
        gathered[h, me1] = acc3[h]

    lane_of = lax.broadcasted_iota(jnp.int32, (FILT, LANES), 1) // GSIZE

    def table(rows8, first, second):
        for g in range(PER_TILE):
            base = jnp.broadcast_to(rows8[g : g + 1, :], (FILT, FILT))
            circ = pltpu.roll(base, 0, 1, stride=1, stride_axis=0).astype(BF16)
            lhs[g * FILT : (g + 1) * FILT, 0:FILT] = circ * masks[first]
            lhs[g * FILT : (g + 1) * FILT, FILT:] = circ * masks[second]

    def apply_table(operand):
        result = jnp.dot(lhs[...], operand, preferred_element_type=F32)
        out = result[0:FILT]
        for g in range(1, PER_TILE):
            out = jnp.where(lane_of == g, result[g * FILT : (g + 1) * FILT], out)
        return out

    def forward(j, carry):
        lanes = lanes_of(j)
        rows8 = rfil[pl.ds(pl.multiple_of(j * PER_TILE, PER_TILE), PER_TILE), :]
        table(rows8, 0, 1)
        conv = apply_table(kvx[j])
        mixed[:, lanes] = (q[:, lanes].astype(F32) * conv).astype(BF16)
        gq[:, lanes] = (dy[:, lanes].astype(F32) * conv).astype(BF16)
        return carry

    def backward(j, carry):
        lanes = lanes_of(j)
        rows8 = fil[pl.ds(pl.multiple_of(j * PER_TILE, PER_TILE), PER_TILE), :]
        table(rows8, 2, 3)
        grad = apply_table(cotx[j])
        gk[:, lanes] = (v[:, lanes].astype(F32) * grad).astype(BF16)
        gv[:, lanes] = (k[:, lanes].astype(F32) * grad).astype(BF16)
        return carry

    def chunks_of(first, end, size, ready, tile_work):
        def one(i, carry):
            ready(i)
            return lax.fori_loop(i * size, (i + 1) * size, tile_work, carry)

        lax.fori_loop(first, end, one, 0)

    def kv_ready(i):
        kv_copy(i).wait_recv()

    def cot_ready(i):
        cot_copy(i).wait_recv()

    def tiles_of(part):
        return (part * tiles) // 16

    def run_forward(first, end):
        lax.fori_loop(tiles_of(first), tiles_of(end), forward, 0)

    def run_backward(first, end):
        chunks_of(tiles_of(first) // COT_CHUNK, tiles_of(end) // COT_CHUNK, COT_CHUNK, cot_ready, backward)

    chunks_of(0, part_chunks, CHUNK, kv_ready, products)
    begin(0)
    hear(0, z_near)
    tell(1, z_far)
    split = part_chunks + part_chunks // 2
    chunks_of(part_chunks, split, CHUNK, kv_ready, products)
    everything(kvs, kv_send, kv_recv.at[0]).wait_send()
    for i in range(n_cot):
        cot_copy(i).start()
    chunks_of(split, n_chunks, CHUNK, kv_ready, products)
    begin(1)
    after1(0)
    hear(1, z_far)
    tell(2, z_far)
    run_forward(0, 6)
    after1(1)
    run_forward(6, 14)
    hear(2, z_far)
    after2(0)
    run_forward(14, 16)
    run_backward(0, 4)
    after2(1)
    run_backward(4, 16)
    after3(0)
    after3(1)
    everything(cots, cot_send, cot_recv.at[0]).wait_send()
    for stage in (stage1, stage2, stage3):
        await_sent(*stage)
    for h in range(PARTS):
        await_part(h, *stage4)
    fg_ref[...] = gathered[...].reshape(fg_ref.shape) * scale
    await_sent(*stage4)


def write_out(*refs):
    *ends, sem = refs
    half = len(ends) // 2
    copies = [
        pltpu.make_async_copy(src, dst, sem.at[i])
        for i, (src, dst) in enumerate(zip(ends[:half], ends[half:]))
    ]
    for copy in copies:
        copy.start()
    for copy in copies:
        copy.wait()


def per_device(n_ctx, n_dp, q_proj, k_proj, v_proj, out_grad, contig_starts, filters):
    rows, width = q_proj.shape[1:]
    groups = filters.shape[0]
    tiles = width // LANES
    n_y = n_ctx // (CORES * Z_LO)
    n_plane = (n_dp // Z_HI) * CORES
    n_z = Z_LO * Z_HI
    share = groups // (n_plane * PARTS)
    n_chunks = tiles // CHUNK
    n_cot = tiles // COT_CHUNK
    scale = 1.0 / math.sqrt(rows * n_ctx * n_dp * GSIZE)
    any_spec = pl.BlockSpec(memory_space=pl.ANY)
    vmem_spec = pl.BlockSpec(memory_space=pltpu.VMEM)
    small = jax.ShapeDtypeStruct((groups, FILT), F32)
    big = jax.ShapeDtypeStruct((rows, width), BF16)
    dma = pltpu.SemaphoreType.DMA
    wide = pltpu.VMEM((rows, width), BF16)
    results = pl.pallas_call(
        functools.partial(ring_kernel, n_ctx, n_dp, scale),
        out_shape=(wide, wide, wide, wide, pltpu.VMEM((groups, FILT), F32)),
        in_specs=[any_spec] * 4 + [vmem_spec] * 2,
        out_specs=(vmem_spec,) * 5,
        scratch_shapes=[
            wide,
            wide,
            wide,
            wide,
            pltpu.VMEM((tiles, 2 * FILT, LANES), BF16),
            pltpu.VMEM((tiles, 2 * FILT, LANES), BF16),
            pltpu.VMEM((tiles, FILT, LANES), BF16),
            pltpu.VMEM((tiles, FILT, LANES), BF16),
            pltpu.VMEM((PER_TILE * FILT, 2 * FILT), BF16),
            pltpu.VMEM((PER_TILE, FILT, LANES), BF16),
            pltpu.VMEM((6, FILT, FILT), BF16),
            pltpu.VMEM((FILT, FILT), F32),
            pltpu.VMEM((groups, FILT), F32),
            pltpu.VMEM((groups, FILT), F32),
            pltpu.VMEM((PER_TILE, SUB, FILT), F32),
            pltpu.VMEM((groups, FILT), F32),
            pltpu.VMEM((groups, FILT), F32),
            pltpu.VMEM((PARTS, n_plane, share, FILT), F32),
            pltpu.VMEM((PARTS, n_y, share, FILT), F32),
            pltpu.VMEM((PARTS, n_z, share, FILT), F32),
            pltpu.VMEM((PARTS, share, FILT), F32),
            pltpu.VMEM((PARTS, share, FILT), F32),
            pltpu.VMEM((PARTS, share, FILT), F32),
            pltpu.VMEM((PARTS, n_plane, share, FILT), F32),
            dma((4,)),
            dma(()),
            dma((n_chunks,)),
            dma(()),
            dma((n_cot,)),
            dma(()),
            dma((PARTS,)),
            dma(()),
            dma((PARTS,)),
            dma(()),
            dma((PARTS,)),
            dma(()),
            dma((PARTS,)),
            pltpu.SemaphoreType.REGULAR((3,)),
        ],
        compiler_params=pltpu.CompilerParams(collective_id=0, has_side_effects=True),
    )(q_proj[0], k_proj[0], v_proj[0], out_grad[0], contig_starts, filters)
    mixed, grad_q, grad_k, grad_v, filter_grad = pl.pallas_call(
        write_out,
        out_shape=(big, big, big, big, small),
        in_specs=[vmem_spec] * 5,
        out_specs=(any_spec,) * 5,
        scratch_shapes=[dma((5,))],
    )(*[pltpu.with_memory_space_constraint(r, pltpu.VMEM) for r in results])
    return (mixed[None], grad_q[None], grad_k[None], grad_v[None], filter_grad)


def solution(mesh):
    split = P("dp", "ctx", None)
    return jax.shard_map(
        functools.partial(per_device, mesh.shape["ctx"], mesh.shape["dp"]),
        mesh=mesh,
        in_specs=(split, split, split, split, P("dp", "ctx"), P()),
        out_specs=(split, split, split, split, P()),
        check_vma=False,
    )
```

```python
import functools
import math

import jax
import jax.numpy as jnp
from jax import lax
from jax.experimental import pallas as pl
from jax.experimental.pallas import tpu as pltpu
from jax.sharding import PartitionSpec as P

FILT = 128
GSIZE = 16
LANES = 128
PER_TILE = LANES // GSIZE
SUB = 8
CORES = 2
Z_LO = 3
Z_HI = 4
CHUNK = 2
COT_CHUNK = 4
PARTS = 2
MESH = pl.DeviceIdType.MESH
F32 = jnp.float32
BF16 = jnp.bfloat16


def ring_kernel(
    n_ctx,
    n_dp,
    scale,
    q_hbm,
    k_hbm,
    v_hbm,
    dy_hbm,
    starts_ref,
    filt_ref,
    mixed,
    gq,
    gk,
    gv,
    fg_ref,
    q,
    k,
    v,
    dy,
    kvx,
    cotx,
    kvs,
    cots,
    lhs,
    apart,
    lane_mask,
    masks,
    pair_mask,
    fil,
    rfil,
    fold,
    filt_rev,
    filt_local,
    slots1,
    slots2,
    slots3,
    acc1,
    acc2,
    acc3,
    gathered,
    in_sem,
    kv_send,
    kv_recv,
    cot_send,
    cot_recv,
    s1_send,
    s1_recv,
    s2_send,
    s2_recv,
    s3_send,
    s3_recv,
    s4_send,
    s4_recv,
    heard,
):
    ctx = lax.axis_index("ctx")
    dp = lax.axis_index("dp")
    core = lax.rem(ctx, CORES)
    z_lo = lax.rem(ctx // CORES, Z_LO)
    y = ctx // (CORES * Z_LO)
    z_hi = lax.rem(dp, Z_HI)
    x = dp // Z_HI
    n_y = n_ctx // (CORES * Z_LO)
    n_x = n_dp // Z_HI
    n_plane = n_x * CORES
    n_z = Z_LO * Z_HI
    me1 = x * CORES + core
    me3 = z_hi * Z_LO + z_lo
    tiles = kvx.shape[0]
    n_chunks = tiles // CHUNK
    n_cot = tiles // COT_CHUNK
    share = filt_local.shape[0] // (n_plane * PARTS)
    part_groups = filt_local.shape[0] // PARTS
    part_chunks = n_chunks // PARTS

    def plane_peer(p):
        return {"ctx": ctx - core + lax.rem(p, CORES), "dp": (p // CORES) * Z_HI + z_hi}

    def y_peer(p):
        return {"ctx": p * (CORES * Z_LO) + z_lo * CORES + core, "dp": dp}

    def z_peer(p):
        return {
            "ctx": y * (CORES * Z_LO) + lax.rem(p, Z_LO) * CORES + core,
            "dp": x * Z_HI + p // Z_LO,
        }

    nxt = {"ctx": lax.rem(ctx + 1, n_ctx), "dp": dp}
    prv = {"ctx": lax.rem(ctx + n_ctx - 1, n_ctx), "dp": dp}

    loads = [
        pltpu.make_async_copy(src, dst, in_sem.at[i])
        for i, (src, dst) in enumerate(((k_hbm, k), (v_hbm, v), (q_hbm, q), (dy_hbm, dy)))
    ]
    for copy in loads:
        copy.start()

    barrier = pltpu.get_barrier_semaphore()

    def greet(device):
        pl.semaphore_signal(barrier, inc=1, device_id=device, device_id_type=MESH)

    def greet_all(n, me, peer):
        def one(d, carry):
            greet(peer(lax.rem(me + d, n)))
            return carry

        lax.fori_loop(1, n, one, 0)

    def z_step(d):
        return z_peer(lax.rem(me3 + d + n_z, n_z))

    def y_step(d):
        return y_peer(lax.rem(y + d + n_y, n_y))

    near = [(z_step, d) for d in (1, -1) if n_z > 1] + [(y_step, d) for d in (1, -1) if n_y > 1]
    far = [(z_step, d) for d in (2, -2) if n_z > 3] + [(y_step, d) for d in (2, -2) if n_y > 3]
    last = [(z_step, d) for d in (2, -2) if n_z > 3]
    greet(nxt)
    greet(prv)
    for step, d in near:
        greet(step(d))
    greet_all(n_plane, me1, plane_peer)

    def tell(stage, steps):
        for step, d in steps:
            pl.semaphore_signal(
                heard.at[stage], inc=1, device_id=step(d), device_id_type=MESH
            )

    def hear(stage, steps):
        if steps:
            pl.semaphore_wait(heard.at[stage], len(steps))

    row = lax.broadcasted_iota(jnp.int32, (FILT, FILT), 0)
    col = lax.broadcasted_iota(jnp.int32, (FILT, FILT), 1)
    starts = starts_ref[...].astype(F32)
    seg_row = jnp.broadcast_to(
        jnp.sum(jnp.where(col <= row, starts, 0.0), axis=1, keepdims=True), (FILT, FILT)
    )
    seg_col = seg_row.T
    starts_sum = jnp.sum(starts)
    same = seg_row == seg_col
    fresh = seg_row == 0.0
    final = seg_row == starts_sum

    def held(cond):
        return jnp.where(cond, 1.0, 0.0)

    low = held(same & (col <= row))
    high = held(fresh & (col > row))
    pair_mask[...] = low + high
    masks[0] = high.astype(BF16)
    masks[1] = low.astype(BF16)
    masks[2] = held(same & (row <= col)).astype(BF16)
    masks[3] = held(final & (col < row)).astype(BF16)
    masks[4] = (held(final) * jnp.where(ctx == n_ctx - 1, 0.0, 1.0)).astype(BF16)
    masks[5] = (held(fresh) * jnp.where(ctx == 0, 0.0, 1.0)).astype(BF16)
    lane_group = col // GSIZE
    for g in range(PER_TILE):
        lane_mask[g] = held(lane_group == g).astype(BF16)
    mirror = held(row == lax.rem(FILT - col, FILT))
    taps = filt_ref[...]
    fil[...] = taps.astype(F32)
    rfil[...] = jnp.dot(taps, mirror.astype(BF16), preferred_element_type=F32)

    def lanes_of(j):
        return pl.ds(pl.multiple_of(j * LANES, LANES), LANES)

    loads[0].wait()
    loads[1].wait()

    def make_kv(j, carry):
        lanes = lanes_of(j)
        prod = (k[:, lanes].astype(F32) * v[:, lanes].astype(F32)).astype(BF16)
        kvx[j, FILT:, :] = prod
        kvs[j] = prod * masks[4]
        return carry

    lax.fori_loop(0, tiles, make_kv, 0)

    pl.semaphore_wait(barrier, 2 + len(near) + (n_plane - 1))

    def kv_copy(i):
        part = pl.ds(i * CHUNK, CHUNK)
        return pltpu.make_async_remote_copy(
            src_ref=kvs.at[part],
            dst_ref=kvx.at[part, 0:FILT, :],
            send_sem=kv_send,
            recv_sem=kv_recv.at[i],
            device_id=nxt,
            device_id_type=MESH,
        )

    def cot_copy(i):
        part = pl.ds(i * COT_CHUNK, COT_CHUNK)
        return pltpu.make_async_remote_copy(
            src_ref=cots.at[part],
            dst_ref=cotx.at[part, FILT:, :],
            send_sem=cot_send,
            recv_sem=cot_recv.at[i],
            device_id=prv,
            device_id_type=MESH,
        )

    for i in range(n_chunks):
        kv_copy(i).start()
    tell(0, near)

    loads[2].wait()
    loads[3].wait()

    def make_cot(j, carry):
        lanes = lanes_of(j)
        prod = (dy[:, lanes].astype(F32) * q[:, lanes].astype(F32)).astype(BF16)
        cotx[j, 0:FILT, :] = prod
        cots[j] = prod * masks[5]
        for g in range(PER_TILE):
            apart[j, g * FILT : (g + 1) * FILT, :] = prod * lane_mask[g]
        return carry

    lax.fori_loop(0, tiles, make_cot, 0)

    def product_tile(j, where):
        pairs = lax.dot_general(
            apart[j], kvx[j], (((1,), (1,)), ((), ())), preferred_element_type=F32
        )
        for g in range(PER_TILE):
            block = pairs[g * FILT : (g + 1) * FILT]
            square = jnp.where(col <= row, block[:, FILT:], block[:, :FILT]) * pair_mask[...]
            folded = square[0:SUB]
            for a in range(1, FILT // SUB):
                folded = folded + pltpu.roll(square[a * SUB : (a + 1) * SUB], FILT - a * SUB, 1)
            fold[where, g] = folded
        taps8 = fold[where, :, 0, :]
        for b in range(1, SUB):
            taps8 = taps8 + pltpu.roll(fold[where, :, b, :], FILT - b, 1)
        filt_rev[pl.ds(pl.multiple_of(j * PER_TILE, PER_TILE), PER_TILE), :] = taps8

    def products(i, carry):
        for where in range(CHUNK):
            product_tile(i * CHUNK + where, where)
        return carry

    def send_all(h, n, me, peer, src_of, dst, landed, send, recv):
        def one(d, carry):
            p = lax.rem(me + d, n)
            pltpu.make_async_remote_copy(
                src_ref=src_of(h, p),
                dst_ref=dst(h, me),
                send_sem=send,
                recv_sem=recv.at[h],
                device_id=peer(p),
                device_id_type=MESH,
            ).start()
            return carry

        lax.fori_loop(1, n, one, 0)

    def everything(part, send, recv):
        return pltpu.make_async_remote_copy(
            src_ref=part,
            dst_ref=part,
            send_sem=send,
            recv_sem=recv,
            device_id=nxt,
            device_id_type=MESH,
        )

    def await_part(h, n, me, peer, src_of, dst, landed, send, recv):
        everything(landed.at[h, pl.ds(0, n - 1)], send, recv.at[h]).wait_recv()

    def await_sent(n, me, peer, src_of, dst, landed, send, recv):
        everything(landed.at[:, pl.ds(0, n - 1)], send, recv.at[0]).wait_send()

    def rows_of(h, p):
        return pl.ds(pl.multiple_of(h * part_groups + p * share, share), share)

    def share_of(ref):
        return lambda h, p: ref.at[rows_of(h, p)]

    def slot_of(ref):
        return lambda h, p: ref.at[h, p]

    def whole(ref):
        return lambda h, p: ref.at[h]

    stage1 = (n_plane, me1, plane_peer, share_of(filt_local), slot_of(slots1), slots1, s1_send, s1_recv)
    stage2 = (n_y, y, y_peer, whole(acc1), slot_of(slots2), slots2, s2_send, s2_recv)
    stage3 = (n_z, me3, z_peer, whole(acc2), slot_of(slots3), slots3, s3_send, s3_recv)
    stage4 = (n_plane, me1, plane_peer, whole(acc3), slot_of(gathered), gathered, s4_send, s4_recv)

    def total(slots, h, n):
        result = slots[h, 0]
        for i in range(1, n):
            result = result + slots[h, i]
        return result

    def begin(h):
        span = slice(h * part_groups, (h + 1) * part_groups)
        filt_local[span, :] = lax.dot_general(
            filt_rev[span, :],
            mirror,
            (((1,), (0,)), ((), ())),
            precision=lax.Precision.HIGHEST,
            preferred_element_type=F32,
        )
        send_all(h, *stage1)
        slots1[h, me1] = filt_local[rows_of(h, me1), :]

    def after1(h):
        await_part(h, *stage1)
        acc1[h] = total(slots1, h, n_plane)
        send_all(h, *stage2)
        slots2[h, y] = acc1[h]

    def after2(h):
        await_part(h, *stage2)
        acc2[h] = total(slots2, h, n_y)
        send_all(h, *stage3)
        slots3[h, me3] = acc2[h]

    def after3(h):
        await_part(h, *stage3)
        acc3[h] = total(slots3, h, n_z)
        send_all(h, *stage4)
        gathered[h, me1] = acc3[h]

    lane_of = lax.broadcasted_iota(jnp.int32, (FILT, LANES), 1) // GSIZE

    def table(rows8, first, second):
        for g in range(PER_TILE):
            base = jnp.broadcast_to(rows8[g : g + 1, :], (FILT, FILT))
            circ = pltpu.roll(base, 0, 1, stride=1, stride_axis=0).astype(BF16)
            lhs[g * FILT : (g + 1) * FILT, 0:FILT] = circ * masks[first]
            lhs[g * FILT : (g + 1) * FILT, FILT:] = circ * masks[second]

    def apply_table(operand):
        result = jnp.dot(lhs[...], operand, preferred_element_type=F32)
        out = result[0:FILT]
        for g in range(1, PER_TILE):
            out = jnp.where(lane_of == g, result[g * FILT : (g + 1) * FILT], out)
        return out

    def forward(j, carry):
        lanes = lanes_of(j)
        rows8 = rfil[pl.ds(pl.multiple_of(j * PER_TILE, PER_TILE), PER_TILE), :]
        table(rows8, 0, 1)
        conv = apply_table(kvx[j])
        mixed[:, lanes] = (q[:, lanes].astype(F32) * conv).astype(BF16)
        gq[:, lanes] = (dy[:, lanes].astype(F32) * conv).astype(BF16)
        return carry

    def backward(j, carry):
        lanes = lanes_of(j)
        rows8 = fil[pl.ds(pl.multiple_of(j * PER_TILE, PER_TILE), PER_TILE), :]
        table(rows8, 2, 3)
        grad = apply_table(cotx[j])
        gk[:, lanes] = (v[:, lanes].astype(F32) * grad).astype(BF16)
        gv[:, lanes] = (k[:, lanes].astype(F32) * grad).astype(BF16)
        return carry

    def chunks_of(first, end, size, ready, tile_work):
        def one(i, carry):
            ready(i)
            return lax.fori_loop(i * size, (i + 1) * size, tile_work, carry)

        lax.fori_loop(first, end, one, 0)

    def kv_ready(i):
        kv_copy(i).wait_recv()

    def cot_ready(i):
        cot_copy(i).wait_recv()

    def tiles_of(part):
        return (part * tiles) // 16

    def run_forward(first, end):
        lax.fori_loop(tiles_of(first), tiles_of(end), forward, 0)

    def run_backward(first, end):
        chunks_of(tiles_of(first) // COT_CHUNK, tiles_of(end) // COT_CHUNK, COT_CHUNK, cot_ready, backward)

    chunks_of(0, part_chunks, 1, kv_ready, products)
    begin(0)
    hear(0, near)
    tell(1, far)
    chunks_of(part_chunks, n_chunks, 1, kv_ready, products)
    begin(1)
    hear(1, far)
    after1(0)
    tell(2, last)
    run_forward(0, 6)
    after1(1)
    for i in range(n_cot):
        cot_copy(i).start()
    run_forward(6, 14)
    hear(2, last)
    after2(0)
    run_forward(14, 16)
    run_backward(0, 4)
    after2(1)
    run_backward(4, 16)
    after3(0)
    after3(1)
    everything(kvs, kv_send, kv_recv.at[0]).wait_send()
    everything(cots, cot_send, cot_recv.at[0]).wait_send()
    for stage in (stage1, stage2, stage3):
        await_sent(*stage)
    for h in range(PARTS):
        await_part(h, *stage4)
    fg_ref[...] = gathered[...].reshape(fg_ref.shape) * scale
    await_sent(*stage4)


def write_out(*refs):
    *ends, sem = refs
    half = len(ends) // 2
    copies = [
        pltpu.make_async_copy(src, dst, sem.at[i])
        for i, (src, dst) in enumerate(zip(ends[:half], ends[half:]))
    ]
    for copy in copies:
        copy.start()
    for copy in copies:
        copy.wait()


def per_device(n_ctx, n_dp, q_proj, k_proj, v_proj, out_grad, contig_starts, filters):
    rows, width = q_proj.shape[1:]
    groups = filters.shape[0]
    tiles = width // LANES
    n_y = n_ctx // (CORES * Z_LO)
    n_plane = (n_dp // Z_HI) * CORES
    n_z = Z_LO * Z_HI
    share = groups // (n_plane * PARTS)
    n_chunks = tiles // CHUNK
    n_cot = tiles // COT_CHUNK
    scale = 1.0 / math.sqrt(rows * n_ctx * n_dp * GSIZE)
    any_spec = pl.BlockSpec(memory_space=pl.ANY)
    vmem_spec = pl.BlockSpec(memory_space=pltpu.VMEM)
    small = jax.ShapeDtypeStruct((groups, FILT), F32)
    big = jax.ShapeDtypeStruct((rows, width), BF16)
    dma = pltpu.SemaphoreType.DMA
    wide = pltpu.VMEM((rows, width), BF16)
    results = pl.pallas_call(
        functools.partial(ring_kernel, n_ctx, n_dp, scale),
        out_shape=(wide, wide, wide, wide, pltpu.VMEM((groups, FILT), F32)),
        in_specs=[any_spec] * 4 + [vmem_spec] * 2,
        out_specs=(vmem_spec,) * 5,
        scratch_shapes=[
            wide,
            wide,
            wide,
            wide,
            pltpu.VMEM((tiles, 2 * FILT, LANES), BF16),
            pltpu.VMEM((tiles, 2 * FILT, LANES), BF16),
            pltpu.VMEM((tiles, FILT, LANES), BF16),
            pltpu.VMEM((tiles, FILT, LANES), BF16),
            pltpu.VMEM((PER_TILE * FILT, 2 * FILT), BF16),
            pltpu.VMEM((tiles, PER_TILE * FILT, LANES), BF16),
            pltpu.VMEM((PER_TILE, FILT, LANES), BF16),
            pltpu.VMEM((6, FILT, FILT), BF16),
            pltpu.VMEM((FILT, FILT), F32),
            pltpu.VMEM((groups, FILT), F32),
            pltpu.VMEM((groups, FILT), F32),
            pltpu.VMEM((CHUNK, PER_TILE, SUB, FILT), F32),
            pltpu.VMEM((groups, FILT), F32),
            pltpu.VMEM((groups, FILT), F32),
            pltpu.VMEM((PARTS, n_plane, share, FILT), F32),
            pltpu.VMEM((PARTS, n_y, share, FILT), F32),
            pltpu.VMEM((PARTS, n_z, share, FILT), F32),
            pltpu.VMEM((PARTS, share, FILT), F32),
            pltpu.VMEM((PARTS, share, FILT), F32),
            pltpu.VMEM((PARTS, share, FILT), F32),
            pltpu.VMEM((PARTS, n_plane, share, FILT), F32),
            dma((4,)),
            dma(()),
            dma((n_chunks,)),
            dma(()),
            dma((n_cot,)),
            dma(()),
            dma((PARTS,)),
            dma(()),
            dma((PARTS,)),
            dma(()),
            dma((PARTS,)),
            dma(()),
            dma((PARTS,)),
            pltpu.SemaphoreType.REGULAR((3,)),
        ],
        compiler_params=pltpu.CompilerParams(collective_id=0, has_side_effects=True),
    )(q_proj[0], k_proj[0], v_proj[0], out_grad[0], contig_starts, filters)
    mixed, grad_q, grad_k, grad_v, filter_grad = pl.pallas_call(
        write_out,
        out_shape=(big, big, big, big, small),
        in_specs=[vmem_spec] * 5,
        out_specs=(any_spec,) * 5,
        scratch_shapes=[dma((5,))],
    )(*[pltpu.with_memory_space_constraint(r, pltpu.VMEM) for r in results])
    return (mixed[None], grad_q[None], grad_k[None], grad_v[None], filter_grad)


def solution(mesh):
    split = P("dp", "ctx", None)
    return jax.shard_map(
        functools.partial(per_device, mesh.shape["ctx"], mesh.shape["dp"]),
        mesh=mesh,
        in_specs=(split, split, split, split, P("dp", "ctx"), P()),
        out_specs=(split, split, split, split, P()),
        check_vma=False,
    )
```

```python
import functools
import math

import jax
import jax.numpy as jnp
from jax import lax
from jax.experimental import pallas as pl
from jax.experimental.pallas import tpu as pltpu
from jax.sharding import PartitionSpec as P

FILT = 128
GSIZE = 16
LANES = 128
PER_TILE = LANES // GSIZE
SUB = 8
CORES = 2
Z_LO = 3
Z_HI = 4
CHUNK = 2
COT_CHUNK = 4
PARTS = 2
MESH = pl.DeviceIdType.MESH
F32 = jnp.float32
BF16 = jnp.bfloat16


def ring_kernel(
    n_ctx,
    n_dp,
    scale,
    q_hbm,
    k_hbm,
    v_hbm,
    dy_hbm,
    starts_ref,
    filt_ref,
    mixed,
    gq,
    gk,
    gv,
    fg_ref,
    q,
    k,
    v,
    dy,
    kvx,
    cotx,
    kvs,
    cots,
    lhs,
    apart,
    lane_mask,
    masks,
    pair_mask,
    fil,
    rfil,
    fold,
    filt_rev,
    filt_local,
    slots1,
    slots2,
    slots3,
    acc1,
    acc2,
    acc3,
    gathered,
    in_sem,
    kv_send,
    kv_recv,
    cot_send,
    cot_recv,
    s1_send,
    s1_recv,
    s2_send,
    s2_recv,
    s3_send,
    s3_recv,
    s4_send,
    s4_recv,
    heard,
):
    ctx = lax.axis_index("ctx")
    dp = lax.axis_index("dp")
    core = lax.rem(ctx, CORES)
    z_lo = lax.rem(ctx // CORES, Z_LO)
    y = ctx // (CORES * Z_LO)
    z_hi = lax.rem(dp, Z_HI)
    x = dp // Z_HI
    n_y = n_ctx // (CORES * Z_LO)
    n_x = n_dp // Z_HI
    n_plane = n_x * CORES
    n_z = Z_LO * Z_HI
    me1 = x * CORES + core
    me3 = z_hi * Z_LO + z_lo
    tiles = kvx.shape[0]
    n_chunks = tiles // CHUNK
    n_cot = tiles // COT_CHUNK
    share = filt_local.shape[0] // (n_plane * PARTS)
    part_groups = filt_local.shape[0] // PARTS
    part_chunks = n_chunks // PARTS

    def plane_peer(p):
        return {"ctx": ctx - core + lax.rem(p, CORES), "dp": (p // CORES) * Z_HI + z_hi}

    def y_peer(p):
        return {"ctx": p * (CORES * Z_LO) + z_lo * CORES + core, "dp": dp}

    def z_peer(p):
        return {
            "ctx": y * (CORES * Z_LO) + lax.rem(p, Z_LO) * CORES + core,
            "dp": x * Z_HI + p // Z_LO,
        }

    nxt = {"ctx": lax.rem(ctx + 1, n_ctx), "dp": dp}
    prv = {"ctx": lax.rem(ctx + n_ctx - 1, n_ctx), "dp": dp}

    loads = [
        pltpu.make_async_copy(src, dst, in_sem.at[i])
        for i, (src, dst) in enumerate(((k_hbm, k), (v_hbm, v), (q_hbm, q), (dy_hbm, dy)))
    ]
    for copy in loads:
        copy.start()

    barrier = pltpu.get_barrier_semaphore()

    def greet(device):
        pl.semaphore_signal(barrier, inc=1, device_id=device, device_id_type=MESH)

    def greet_all(n, me, peer):
        def one(d, carry):
            greet(peer(lax.rem(me + d, n)))
            return carry

        lax.fori_loop(1, n, one, 0)

    def z_step(d):
        return z_peer(lax.rem(me3 + d + n_z, n_z))

    def y_step(d):
        return y_peer(lax.rem(y + d + n_y, n_y))

    near = [(z_step, d) for d in (1, -1) if n_z > 1] + [(y_step, d) for d in (1, -1) if n_y > 1]
    far = [(z_step, d) for d in (2, -2) if n_z > 3] + [(y_step, d) for d in (2, -2) if n_y > 3]
    last = [(z_step, d) for d in (2, -2) if n_z > 3]
    greet(nxt)
    greet(prv)
    for step, d in near:
        greet(step(d))
    greet_all(n_plane, me1, plane_peer)

    def tell(stage, steps):
        for step, d in steps:
            pl.semaphore_signal(
                heard.at[stage], inc=1, device_id=step(d), device_id_type=MESH
            )

    def hear(stage, steps):
        if steps:
            pl.semaphore_wait(heard.at[stage], len(steps))

    row = lax.broadcasted_iota(jnp.int32, (FILT, FILT), 0)
    col = lax.broadcasted_iota(jnp.int32, (FILT, FILT), 1)
    starts = starts_ref[...].astype(F32)
    seg_row = jnp.broadcast_to(
        jnp.sum(jnp.where(col <= row, starts, 0.0), axis=1, keepdims=True), (FILT, FILT)
    )
    seg_col = seg_row.T
    starts_sum = jnp.sum(starts)
    same = seg_row == seg_col
    fresh = seg_row == 0.0
    final = seg_row == starts_sum

    def held(cond):
        return jnp.where(cond, 1.0, 0.0)

    low = held(same & (col <= row))
    high = held(fresh & (col > row))
    pair_mask[...] = low + high
    masks[0] = high.astype(BF16)
    masks[1] = low.astype(BF16)
    masks[2] = held(same & (row <= col)).astype(BF16)
    masks[3] = held(final & (col < row)).astype(BF16)
    masks[4] = (held(final) * jnp.where(ctx == n_ctx - 1, 0.0, 1.0)).astype(BF16)
    masks[5] = (held(fresh) * jnp.where(ctx == 0, 0.0, 1.0)).astype(BF16)
    lane_group = col // GSIZE
    for g in range(PER_TILE):
        lane_mask[g] = held(lane_group == g).astype(BF16)
    mirror = held(row == lax.rem(FILT - col, FILT))
    taps = filt_ref[...]
    fil[...] = taps.astype(F32)
    rfil[...] = jnp.dot(taps, mirror.astype(BF16), preferred_element_type=F32)

    def lanes_of(j):
        return pl.ds(pl.multiple_of(j * LANES, LANES), LANES)

    loads[0].wait()
    loads[1].wait()

    def make_kv(j, carry):
        lanes = lanes_of(j)
        prod = (k[:, lanes].astype(F32) * v[:, lanes].astype(F32)).astype(BF16)
        kvx[j, FILT:, :] = prod
        kvs[j] = prod * masks[4]
        return carry

    lax.fori_loop(0, tiles, make_kv, 0)

    pl.semaphore_wait(barrier, 2 + len(near) + (n_plane - 1))

    def kv_copy(i):
        part = pl.ds(i * CHUNK, CHUNK)
        return pltpu.make_async_remote_copy(
            src_ref=kvs.at[part],
            dst_ref=kvx.at[part, 0:FILT, :],
            send_sem=kv_send,
            recv_sem=kv_recv.at[i],
            device_id=nxt,
            device_id_type=MESH,
        )

    def cot_copy(i):
        part = pl.ds(i * COT_CHUNK, COT_CHUNK)
        return pltpu.make_async_remote_copy(
            src_ref=cots.at[part],
            dst_ref=cotx.at[part, FILT:, :],
            send_sem=cot_send,
            recv_sem=cot_recv.at[i],
            device_id=prv,
            device_id_type=MESH,
        )

    for i in range(n_chunks):
        kv_copy(i).start()
    tell(0, near)

    loads[2].wait()
    loads[3].wait()

    def make_cot(j, carry):
        lanes = lanes_of(j)
        prod = (dy[:, lanes].astype(F32) * q[:, lanes].astype(F32)).astype(BF16)
        cotx[j, 0:FILT, :] = prod
        cots[j] = prod * masks[5]
        for g in range(PER_TILE):
            apart[j, g * FILT : (g + 1) * FILT, :] = prod * lane_mask[g]
        return carry

    lax.fori_loop(0, tiles, make_cot, 0)

    def product_tile(j, where):
        pairs = lax.dot_general(
            apart[j], kvx[j], (((1,), (1,)), ((), ())), preferred_element_type=F32
        )
        for g in range(PER_TILE):
            block = pairs[g * FILT : (g + 1) * FILT]
            square = jnp.where(col <= row, block[:, FILT:], block[:, :FILT]) * pair_mask[...]
            folded = square[0:SUB]
            for a in range(1, FILT // SUB):
                folded = folded + pltpu.roll(square[a * SUB : (a + 1) * SUB], FILT - a * SUB, 1)
            fold[where, g] = folded
        taps8 = fold[where, :, 0, :]
        for b in range(1, SUB):
            taps8 = taps8 + pltpu.roll(fold[where, :, b, :], FILT - b, 1)
        filt_rev[pl.ds(pl.multiple_of(j * PER_TILE, PER_TILE), PER_TILE), :] = taps8

    def products(i, carry):
        for where in range(CHUNK):
            product_tile(i * CHUNK + where, where)
        return carry

    def send_all(h, n, me, peer, src_of, dst, landed, send, recv):
        def one(d, carry):
            p = lax.rem(me + d, n)
            pltpu.make_async_remote_copy(
                src_ref=src_of(h, p),
                dst_ref=dst(h, me),
                send_sem=send,
                recv_sem=recv.at[h],
                device_id=peer(p),
                device_id_type=MESH,
            ).start()
            return carry

        lax.fori_loop(1, n, one, 0)

    def everything(part, send, recv):
        return pltpu.make_async_remote_copy(
            src_ref=part,
            dst_ref=part,
            send_sem=send,
            recv_sem=recv,
            device_id=nxt,
            device_id_type=MESH,
        )

    def await_part(h, n, me, peer, src_of, dst, landed, send, recv):
        everything(landed.at[h, pl.ds(0, n - 1)], send, recv.at[h]).wait_recv()

    def await_sent(n, me, peer, src_of, dst, landed, send, recv):
        everything(landed.at[:, pl.ds(0, n - 1)], send, recv.at[0]).wait_send()

    def rows_of(h, p):
        return pl.ds(pl.multiple_of(h * part_groups + p * share, share), share)

    def share_of(ref):
        return lambda h, p: ref.at[rows_of(h, p)]

    def slot_of(ref):
        return lambda h, p: ref.at[h, p]

    def whole(ref):
        return lambda h, p: ref.at[h]

    stage1 = (n_plane, me1, plane_peer, share_of(filt_local), slot_of(slots1), slots1, s1_send, s1_recv)
    stage2 = (n_y, y, y_peer, whole(acc1), slot_of(slots2), slots2, s2_send, s2_recv)
    stage3 = (n_z, me3, z_peer, whole(acc2), slot_of(slots3), slots3, s3_send, s3_recv)
    stage4 = (n_plane, me1, plane_peer, whole(acc3), slot_of(gathered), gathered, s4_send, s4_recv)

    def total(slots, h, n):
        result = slots[h, 0]
        for i in range(1, n):
            result = result + slots[h, i]
        return result

    def begin(h):
        span = slice(h * part_groups, (h + 1) * part_groups)
        filt_local[span, :] = lax.dot_general(
            filt_rev[span, :],
            mirror,
            (((1,), (0,)), ((), ())),
            precision=lax.Precision.HIGHEST,
            preferred_element_type=F32,
        )
        send_all(h, *stage1)
        slots1[h, me1] = filt_local[rows_of(h, me1), :]

    def after1(h):
        await_part(h, *stage1)
        acc1[h] = total(slots1, h, n_plane)
        send_all(h, *stage2)
        slots2[h, y] = acc1[h]

    def after2(h):
        await_part(h, *stage2)
        acc2[h] = total(slots2, h, n_y)
        send_all(h, *stage3)
        slots3[h, me3] = acc2[h]

    def after3(h):
        await_part(h, *stage3)
        acc3[h] = total(slots3, h, n_z)
        send_all(h, *stage4)
        gathered[h, me1] = acc3[h]

    lane_of = lax.broadcasted_iota(jnp.int32, (FILT, LANES), 1) // GSIZE

    def table(rows8, first, second):
        for g in range(PER_TILE):
            base = jnp.broadcast_to(rows8[g : g + 1, :], (FILT, FILT))
            circ = pltpu.roll(base, 0, 1, stride=1, stride_axis=0).astype(BF16)
            lhs[g * FILT : (g + 1) * FILT, 0:FILT] = circ * masks[first]
            lhs[g * FILT : (g + 1) * FILT, FILT:] = circ * masks[second]

    def apply_table(operand):
        result = jnp.dot(lhs[...], operand, preferred_element_type=F32)
        out = result[0:FILT]
        for g in range(1, PER_TILE):
            out = jnp.where(lane_of == g, result[g * FILT : (g + 1) * FILT], out)
        return out

    def forward(j, carry):
        lanes = lanes_of(j)
        rows8 = rfil[pl.ds(pl.multiple_of(j * PER_TILE, PER_TILE), PER_TILE), :]
        table(rows8, 0, 1)
        conv = apply_table(kvx[j])
        mixed[:, lanes] = (q[:, lanes].astype(F32) * conv).astype(BF16)
        gq[:, lanes] = (dy[:, lanes].astype(F32) * conv).astype(BF16)
        return carry

    def backward(j, carry):
        lanes = lanes_of(j)
        rows8 = fil[pl.ds(pl.multiple_of(j * PER_TILE, PER_TILE), PER_TILE), :]
        table(rows8, 2, 3)
        grad = apply_table(cotx[j])
        gk[:, lanes] = (v[:, lanes].astype(F32) * grad).astype(BF16)
        gv[:, lanes] = (k[:, lanes].astype(F32) * grad).astype(BF16)
        return carry

    def chunks_of(first, end, size, ready, tile_work):
        def one(i, carry):
            ready(i)
            return lax.fori_loop(i * size, (i + 1) * size, tile_work, carry)

        lax.fori_loop(first, end, one, 0)

    def kv_ready(i):
        kv_copy(i).wait_recv()

    def cot_ready(i):
        cot_copy(i).wait_recv()

    def tiles_of(part):
        return (part * tiles) // 16

    def run_forward(first, end):
        lax.fori_loop(tiles_of(first), tiles_of(end), forward, 0)

    def run_backward(first, end):
        chunks_of(tiles_of(first) // COT_CHUNK, tiles_of(end) // COT_CHUNK, COT_CHUNK, cot_ready, backward)

    chunks_of(0, part_chunks, 1, kv_ready, products)
    begin(0)
    hear(0, near)
    tell(1, far)
    chunks_of(part_chunks, n_chunks, 1, kv_ready, products)
    begin(1)
    hear(1, far)
    after1(0)
    tell(2, last)
    run_forward(0, 5)
    after1(1)
    for i in range(n_cot):
        cot_copy(i).start()
    run_forward(5, 11)
    hear(2, last)
    after2(0)
    run_forward(11, 14)
    after2(1)
    run_forward(14, 16)
    run_backward(0, 16)
    after3(0)
    after3(1)
    everything(kvs, kv_send, kv_recv.at[0]).wait_send()
    everything(cots, cot_send, cot_recv.at[0]).wait_send()
    for stage in (stage1, stage2, stage3):
        await_sent(*stage)
    for h in range(PARTS):
        await_part(h, *stage4)
    fg_ref[...] = gathered[...].reshape(fg_ref.shape) * scale
    await_sent(*stage4)


def write_out(*refs):
    *ends, sem = refs
    half = len(ends) // 2
    copies = [
        pltpu.make_async_copy(src, dst, sem.at[i])
        for i, (src, dst) in enumerate(zip(ends[:half], ends[half:]))
    ]
    for copy in copies:
        copy.start()
    for copy in copies:
        copy.wait()


def per_device(n_ctx, n_dp, q_proj, k_proj, v_proj, out_grad, contig_starts, filters):
    rows, width = q_proj.shape[1:]
    groups = filters.shape[0]
    tiles = width // LANES
    n_y = n_ctx // (CORES * Z_LO)
    n_plane = (n_dp // Z_HI) * CORES
    n_z = Z_LO * Z_HI
    share = groups // (n_plane * PARTS)
    n_chunks = tiles // CHUNK
    n_cot = tiles // COT_CHUNK
    scale = 1.0 / math.sqrt(rows * n_ctx * n_dp * GSIZE)
    any_spec = pl.BlockSpec(memory_space=pl.ANY)
    vmem_spec = pl.BlockSpec(memory_space=pltpu.VMEM)
    small = jax.ShapeDtypeStruct((groups, FILT), F32)
    big = jax.ShapeDtypeStruct((rows, width), BF16)
    dma = pltpu.SemaphoreType.DMA
    wide = pltpu.VMEM((rows, width), BF16)
    results = pl.pallas_call(
        functools.partial(ring_kernel, n_ctx, n_dp, scale),
        out_shape=(wide, wide, wide, wide, pltpu.VMEM((groups, FILT), F32)),
        in_specs=[any_spec] * 4 + [vmem_spec] * 2,
        out_specs=(vmem_spec,) * 5,
        scratch_shapes=[
            wide,
            wide,
            wide,
            wide,
            pltpu.VMEM((tiles, 2 * FILT, LANES), BF16),
            pltpu.VMEM((tiles, 2 * FILT, LANES), BF16),
            pltpu.VMEM((tiles, FILT, LANES), BF16),
            pltpu.VMEM((tiles, FILT, LANES), BF16),
            pltpu.VMEM((PER_TILE * FILT, 2 * FILT), BF16),
            pltpu.VMEM((tiles, PER_TILE * FILT, LANES), BF16),
            pltpu.VMEM((PER_TILE, FILT, LANES), BF16),
            pltpu.VMEM((6, FILT, FILT), BF16),
            pltpu.VMEM((FILT, FILT), F32),
            pltpu.VMEM((groups, FILT), F32),
            pltpu.VMEM((groups, FILT), F32),
            pltpu.VMEM((CHUNK, PER_TILE, SUB, FILT), F32),
            pltpu.VMEM((groups, FILT), F32),
            pltpu.VMEM((groups, FILT), F32),
            pltpu.VMEM((PARTS, n_plane, share, FILT), F32),
            pltpu.VMEM((PARTS, n_y, share, FILT), F32),
            pltpu.VMEM((PARTS, n_z, share, FILT), F32),
            pltpu.VMEM((PARTS, share, FILT), F32),
            pltpu.VMEM((PARTS, share, FILT), F32),
            pltpu.VMEM((PARTS, share, FILT), F32),
            pltpu.VMEM((PARTS, n_plane, share, FILT), F32),
            dma((4,)),
            dma(()),
            dma((n_chunks,)),
            dma(()),
            dma((n_cot,)),
            dma(()),
            dma((PARTS,)),
            dma(()),
            dma((PARTS,)),
            dma(()),
            dma((PARTS,)),
            dma(()),
            dma((PARTS,)),
            pltpu.SemaphoreType.REGULAR((3,)),
        ],
        compiler_params=pltpu.CompilerParams(collective_id=0, has_side_effects=True),
    )(q_proj[0], k_proj[0], v_proj[0], out_grad[0], contig_starts, filters)
    mixed, grad_q, grad_k, grad_v, filter_grad = pl.pallas_call(
        write_out,
        out_shape=(big, big, big, big, small),
        in_specs=[vmem_spec] * 5,
        out_specs=(any_spec,) * 5,
        scratch_shapes=[dma((5,))],
    )(*[pltpu.with_memory_space_constraint(r, pltpu.VMEM) for r in results])
    return (mixed[None], grad_q[None], grad_k[None], grad_v[None], filter_grad)


def solution(mesh):
    split = P("dp", "ctx", None)
    return jax.shard_map(
        functools.partial(per_device, mesh.shape["ctx"], mesh.shape["dp"]),
        mesh=mesh,
        in_specs=(split, split, split, split, P("dp", "ctx"), P()),
        out_specs=(split, split, split, split, P()),
        check_vma=False,
    )
```
